32 devices in a mesh: cube: 2 (over y), row: 4 (over x, core), col: 4 (over z).
Axes of the slice: x: 2, y: 2, z: 4, core: 2. Of those that a mesh axis runs over, the one named last changes fastest.
Arguments:
- child_panel: bfloat16 [2, 6144, 256], P('cube', ('row', 'col')), may hold values from -0.75 to 0.75
- child_inverse: float32 [2, 256, 256], P('cube')
- child_trailing: bfloat16 [2, 6144, 6144], P('cube', ('row', 'col')), may hold values from -6 to 6
- child_pattern: int32 [2, 48], P('cube'), may hold values 0 or 1
- child_map: int32 [2, 48], replicated, may hold values from 0 to 95, as said below
- parent_panel: bfloat16 [2, 6144, 256], P('cube', ('row', 'col')), may hold values from -0.75 to 0.75
- parent_inverse: float32 [1, 256, 256], replicated
- parent_trailing: bfloat16 [2, 6144, 12288], P('cube', ('row', 'col')), may hold values from -6 to 6
- parent_pattern: int32 [1, 96], replicated, may hold values 0 or 1
Outputs:
- parent_update: bfloat16 [2, 6144, 12288], P('cube', ('row', 'col'))
The draws below stay inside these ranges and needn't reach their ends.
Inputs may be any that keep to these rules, and one draw needn't show every extreme that they name: With p = i // 3, child_map[c, i] is one of the blocks h * 48 + p * 3 + k, h in 0 and 1, k from 0 to 2; a child's blocks land on distinct parent blocks.
All inputs are finite; a program needn't handle non-finite values. No bound on the sum of `child_pattern` on one device may be relied on, other than what follows from the above.
Results may differ from the reference program's by a relative error of at most 0.0042.
Values may be sent and summed in bfloat16 or wider, within the bound.
No kernel may reach another device: no remote copies, remote signals or barrier semaphores. Data moves between devices by JAX's collectives and lax.ppermute only.
A program may use at most 192 MiB of HBM per device.

```python
import math
import jax
import jax.numpy as jnp
from jax import lax

BLOCK = 128
PIVOTS = 256
CHILD_BLOCKS = 48
PARENT_BLOCKS = 96
POSITIONS = 16
CHILD_ORDER = 6144
PARENT_ORDER = 12288
PARENT_HALF = 6144
CHILDREN = 2
PARENTS = 1


def symmetric_draw(key, how_many):
    first_key, second_key = jax.random.split(key, 2)
    identity = jnp.eye(PIVOTS, dtype=jnp.float32)
    diagonal = jnp.exp(jax.random.uniform(first_key, (how_many, PIVOTS), jnp.float32, math.log(0.5), math.log(2.0)))
    noise_draw = jax.random.normal(second_key, (how_many, PIVOTS, PIVOTS), jnp.float32)
    off_part = (noise_draw + jnp.swapaxes(noise_draw, 1, 2)) * (0.15 / math.sqrt(PIVOTS))
    matrix = off_part * (1.0 - identity) + identity * diagonal[:, :, None]
    return matrix.astype(jnp.float32)


def draw_child_inverse(key, part):
    return symmetric_draw(jax.random.fold_in(key, 3), CHILDREN)


def draw_parent_inverse(key, part):
    return symmetric_draw(jax.random.fold_in(key, 5), PARENTS)


def draw_child_map(key, part):
    per_device = CHILD_BLOCKS // POSITIONS
    window = PARENT_BLOCKS // (2 * POSITIONS)
    half_blocks = PARENT_BLOCKS // 2
    subkeys = jax.random.split(jax.random.fold_in(key, 11), CHILDREN * POSITIONS)
    places = jnp.tile(jnp.arange(POSITIONS, dtype=jnp.int32), CHILDREN)

    def single_window(subkey, place):
        ranks = jax.random.permutation(subkey, 2 * window).astype(jnp.int32)
        candidates = jnp.arange(2 * window, dtype=jnp.int32)
        forced = jnp.where(place == 0, 0, 2 * window - 1).astype(jnp.int32)
        needed = (place == 0) | (place == POSITIONS - 1)
        scores = jnp.where(needed & (candidates == forced), -1, ranks).astype(jnp.int32)
        picked = jnp.sort(jnp.argsort(scores, stable=True)[:per_device].astype(jnp.int32))
        halves = picked // window
        return (halves * half_blocks + place * window + picked % window).astype(jnp.int32)
    chosen = jax.vmap(single_window)(subkeys, places)
    return chosen.reshape(CHILDREN, POSITIONS * per_device).astype(jnp.int32)


def with_ends(array, stream_key, least, largest):
    longest = array.shape.index(max(array.shape))
    spots = []
    for shift in (0, 1):
        where = [jax.random.randint(jax.random.fold_in(stream_key, axis), (), 0, length) for axis, length in enumerate(array.shape)]
        where[longest] = (where[longest] + shift) % array.shape[longest]
        spots.append(tuple(where))
    return array.at[spots[0]].set(least).at[spots[1]].set(largest)


def level_of(own_key, shape, pieces, low, largest):
    level, own = 1.0, jax.random.fold_in(own_key, 6)
    for dim, parts in pieces:
        heights = jnp.exp(jax.random.uniform(jax.random.fold_in(own, dim), (parts,), jnp.float32, low / len(pieces), largest / len(pieces)))
        level = level * jnp.repeat(heights, shape[dim] // parts).reshape([-1 if axis == dim else 1 for axis in range(len(shape))])
    return level


def bell_draw(own_key, extent, scale, most, cuts=(), kind=jnp.bfloat16):
    entries = jax.random.normal(own_key, extent, jnp.float32) * scale
    if len(cuts) > 0:
        entries = level_of(own_key, extent, cuts, -0.22, 0.18) * entries
    return jnp.clip(entries, min=-most, max=most).astype(kind)


def setup_inputs(seed: int = 0) -> dict:
    seeds = jax.random.split(jax.random.key(seed), 10)
    child_panel = bell_draw(seeds[0], (CHILDREN, CHILD_ORDER, PIVOTS), 0.125, 0.75, ((0, 2), (1, 16)))
    child_inverse = draw_child_inverse(jax.random.fold_in(seeds[9], 71), 0)
    child_trailing = bell_draw(seeds[2], (CHILDREN, CHILD_ORDER, CHILD_ORDER), 1.0, 6.0, ((0, 2), (1, 16)))
    child_pattern = with_ends((jax.random.randint(seeds[3], (CHILDREN, CHILD_BLOCKS), 0, 4) < 3).astype(jnp.int32), jax.random.fold_in(seeds[3], 1), 0, 1)
    child_map = draw_child_map(jax.random.fold_in(seeds[9], 71), 0)
    parent_panel = bell_draw(seeds[5], (CHILDREN, PARENT_HALF, PIVOTS), 0.125, 0.75, ((0, 2), (1, 16)))
    parent_inverse = draw_parent_inverse(jax.random.fold_in(seeds[9], 71), 0)
    parent_trailing = bell_draw(seeds[7], (CHILDREN, PARENT_HALF, PARENT_ORDER), 1.0, 6.0, ((0, 2), (1, 16)))
    parent_pattern = with_ends((jax.random.randint(seeds[8], (PARENTS, PARENT_BLOCKS), 0, 4) < 3).astype(jnp.int32), jax.random.fold_in(seeds[8], 1), 0, 1)
    return dict(child_panel=child_panel, child_inverse=child_inverse, child_trailing=child_trailing, child_pattern=child_pattern, child_map=child_map, parent_panel=parent_panel, parent_inverse=parent_inverse, parent_trailing=parent_trailing, parent_pattern=parent_pattern)


def mask_rows(panel_rows, pattern):
    return panel_rows * jnp.repeat(pattern, BLOCK).astype(panel_rows.dtype)[:, None]


def reduced(trailing, panel_rows, pattern, inverse):
    masked = mask_rows(panel_rows, pattern)
    left_factor = jnp.dot(masked.astype(jnp.float32), inverse, precision=lax.Precision.HIGHEST).astype(jnp.bfloat16)
    update = lax.dot_general(left_factor, masked, (((1,), (1,)), ((), ())), preferred_element_type=jnp.float32)
    return trailing.astype(jnp.float32) - update


def reference(child_panel, child_inverse, child_trailing, child_pattern, child_map, parent_panel, parent_inverse, parent_trailing, parent_pattern):
    offsets = jnp.arange(BLOCK, dtype=jnp.int32)
    halves = []
    for parent in range(PARENTS):
        assembled = jnp.zeros((PARENT_ORDER, PARENT_ORDER), jnp.float32)
        for offspring in (2 * parent, 2 * parent + 1):
            schur_block = reduced(child_trailing[offspring], child_panel[offspring], child_pattern[offspring], child_inverse[offspring]).astype(jnp.bfloat16)
            places = (child_map[offspring].astype(jnp.int32)[:, None] * BLOCK + offsets[None, :]).reshape(-1).astype(jnp.int32)
            assembled = assembled.at[places[:, None], places[None, :]].add(schur_block.astype(jnp.float32))
        assembled = assembled.astype(jnp.bfloat16)
        panel_rows = jnp.concatenate([parent_panel[2 * parent], parent_panel[2 * parent + 1]], axis=0)
        trailing = jnp.concatenate([parent_trailing[2 * parent], parent_trailing[2 * parent + 1]], axis=0)
        whole = reduced(trailing, panel_rows, parent_pattern[parent], parent_inverse[parent]) + assembled.astype(jnp.float32)
        whole = whole.astype(jnp.bfloat16)
        halves.append(whole[:PARENT_HALF])
        halves.append(whole[PARENT_HALF:])
    return jnp.stack(halves)
```

```python
import functools
import jax
import jax.numpy as jnp
from jax import lax
from jax.experimental import pallas as pl
from jax.experimental.pallas import tpu as pltpu
from jax.sharding import PartitionSpec as P

BLOCK = 128


def swap_cube(array):
    return lax.ppermute(array, "cube", [(i, i ^ 1) for i in range(lax.axis_size("cube"))])


def masked_rows(panel, pattern_row, start):
    blocks = panel.shape[0] // BLOCK
    window = lax.dynamic_slice_in_dim(pattern_row, start, blocks)
    return panel * jnp.repeat(window, BLOCK).astype(panel.dtype)[:, None]


def left_factor(masked, inverse):
    return jnp.dot(masked.astype(jnp.float32), inverse, precision=lax.Precision.HIGHEST).astype(jnp.bfloat16)


def source_table(mapping, positions, parent_blocks):
    each = mapping.shape[0] // positions
    width = parent_blocks // (2 * positions)
    target = jnp.arange(parent_blocks, dtype=jnp.int32).reshape(2, positions, width)
    hit = mapping.reshape(1, positions, 1, each) == target[..., None]
    return jnp.sum(jnp.where(hit, jnp.arange(1, each + 1, dtype=jnp.int32), 0), axis=-1) - 1


def assemble_chunk(first, windows, per_step, positions, each, width, table, place, lefts, gathered, own, other, trailing, previous):
    rows = own.shape[0]
    span = each * BLOCK
    wide = width * BLOCK
    row_blocks = rows // BLOCK
    zero = row_blocks * each
    steps = windows // per_step

    def kernel(table_ref, place_ref, lefts_ref, gathered_ref, own_ref, other_ref, trailing_ref, *rest):
        out_ref, schur_ref = rest[-2:]
        step = pl.program_id(0)
        half = pl.program_id(1)

        def source(child, which_half, window, k):
            return table_ref[((child * 2 + which_half) * positions + window) * width + k]

        @pl.when(half == 0)
        def _():
            for child, piece in enumerate((own_ref, other_ref)):
                for j in range(per_step):
                    update = lax.dot_general(
                        lefts_ref[child], gathered_ref[j, 2 * child], (((1,), (1,)), ((), ())),
                        preferred_element_type=jnp.float32,
                    )
                    schur = (piece[:, j * span:(j + 1) * span].astype(jnp.float32) - update).astype(jnp.bfloat16)
                    for r in range(row_blocks):
                        for c in range(each):
                            schur_ref[child, j, r * each + c] = schur[r * BLOCK:(r + 1) * BLOCK, c * BLOCK:(c + 1) * BLOCK]
                    schur_ref[child, j, zero] = jnp.zeros((BLOCK, BLOCK), jnp.bfloat16)

        own_half = place_ref[0]
        position = place_ref[1]
        slot = jnp.where(half == own_half, 1, 3)
        for j in range(per_step):
            window = first + step * per_step + j
            update = lax.dot_general(
                lefts_ref[2], gathered_ref[j, slot], (((1,), (1,)), ((), ())), preferred_element_type=jnp.float32
            )
            base = trailing_ref[:, j * wide:(j + 1) * wide].astype(jnp.float32) - update
            for a in range(row_blocks):
                for k in range(width):
                    total = None
                    for child in range(2):
                        r = source(child, own_half, position, a)
                        c = source(child, half, window, k)
                        which = jnp.where((r >= 0) & (c >= 0), r * each + c, zero)
                        block = schur_ref[child, j, which].astype(jnp.float32)
                        total = block if total is None else total + block
                    total = total.astype(jnp.bfloat16).astype(jnp.float32)
                    piece = base[a * BLOCK:(a + 1) * BLOCK, k * BLOCK:(k + 1) * BLOCK] + total
                    at = j * wide + k * BLOCK
                    out_ref[a * BLOCK:(a + 1) * BLOCK, at:at + BLOCK] = piece.astype(jnp.bfloat16)

    start = first // per_step
    halves = positions // per_step
    smem = pl.BlockSpec(memory_space=pltpu.SMEM)
    in_specs = [
        smem,
        smem,
        pl.BlockSpec(lefts.shape, lambda s, h: (0, 0, 0)),
        pl.BlockSpec((per_step,) + gathered.shape[1:], lambda s, h: (start + s, 0, 0, 0)),
        pl.BlockSpec((rows, per_step * span), lambda s, h: (0, start + s)),
        pl.BlockSpec((rows, per_step * span), lambda s, h: (0, s)),
        pl.BlockSpec((rows, per_step * wide), lambda s, h: (0, h * halves + start + s)),
    ]
    operands = [table, place, lefts, gathered, own, other, trailing]
    aliases = {}
    if previous is not None:
        in_specs.append(pl.BlockSpec(memory_space=pl.ANY))
        operands.append(previous)
        aliases = {len(operands) - 1: 0}
    return pl.pallas_call(
        kernel,
        grid=(steps, 2),
        in_specs=in_specs,
        out_specs=pl.BlockSpec((rows, per_step * wide), lambda s, h: (0, h * halves + start + s)),
        out_shape=jax.ShapeDtypeStruct(trailing.shape, jnp.bfloat16),
        scratch_shapes=[pltpu.VMEM((2, per_step, zero + 1, BLOCK, BLOCK), jnp.bfloat16)],
        input_output_aliases=aliases,
        name="assemble",
        compiler_params=pltpu.CompilerParams(vmem_limit_bytes=32 * 1024 * 1024),
    )(*operands)


def local(
    child_panel,
    child_inverse,
    child_trailing,
    child_pattern,
    child_map,
    parent_panel,
    parent_inverse,
    parent_trailing,
    parent_pattern,
):
    positions = lax.axis_size(("row", "col"))
    position = lax.axis_index(("row", "col"))
    cube_index = lax.axis_index("cube")
    half_bit = cube_index % 2
    parent = cube_index // 2
    parent_blocks = parent_pattern.shape[1]
    child_blocks = child_map.shape[1]
    each = child_blocks // positions
    width = parent_blocks // (2 * positions)
    own = child_trailing[0]
    rows = own.shape[0]
    span = each * BLOCK

    own_child = masked_rows(child_panel[0], child_pattern[0], position * each)
    pattern_row = lax.dynamic_index_in_dim(parent_pattern, parent, 0, keepdims=False)
    own_parent = masked_rows(parent_panel[0], pattern_row, half_bit * (parent_blocks // 2) + position * width)
    child_left = left_factor(own_child, child_inverse[0])
    parent_left = left_factor(own_parent, lax.dynamic_index_in_dim(parent_inverse, parent, 0, keepdims=False))

    small = jnp.stack([own_child, own_parent, child_left])
    small_other = swap_cube(small)

    per_step = 2
    sizes = [4, 4, 4, 2, 2] if positions == 16 else [positions]
    others, first = [], 0
    for size in sizes:
        others.append(swap_cube(own[:, first * span:(first + size) * span]))
        first += size

    pieces = jnp.concatenate([small[:2], small_other[:2]])
    gathered = lax.all_gather(pieces, ("row", "col"), axis=0, tiled=False)
    lefts = jnp.stack([child_left, small_other[2], parent_left])

    own_map = lax.dynamic_index_in_dim(child_map, cube_index, 0, keepdims=False)
    other_map = lax.dynamic_index_in_dim(child_map, cube_index ^ 1, 0, keepdims=False)
    table = jnp.stack([source_table(m, positions, parent_blocks) for m in (own_map, other_map)]).reshape(-1)
    place = jnp.stack([half_bit, position]).astype(jnp.int32)

    result, first = None, 0
    for size, other in zip(sizes, others):
        result = assemble_chunk(
            first, size, per_step, positions, each, width, table, place, lefts, gathered, own, other, parent_trailing[0], result
        )
        first += size
    return result[None]


def solution(mesh):
    in_specs = (
        P("cube", ("row", "col"), None),
        P("cube", None, None),
        P("cube", ("row", "col"), None),
        P("cube", None),
        P(),
        P("cube", ("row", "col"), None),
        P(),
        P("cube", ("row", "col"), None),
        P(),
    )
    out_specs = P("cube", ("row", "col"), None)
    return jax.shard_map(local, mesh=mesh, in_specs=in_specs, out_specs=out_specs, check_vma=False)
```

```python
import jax
import jax.numpy as jnp
from jax import lax
from jax.experimental import pallas as pl
from jax.experimental.pallas import tpu as pltpu
from jax.sharding import PartitionSpec as P

BLOCK = 128


def swap(array, axis, bit):
    return lax.ppermute(array, axis, [(i, i ^ 1 << bit) for i in range(lax.axis_size(axis))])


def shift(array, axis, by):
    extent = lax.axis_size(axis)
    return lax.ppermute(array, axis, [(i, (i + by) % extent) for i in range(extent)])


def masked_rows(panel, pattern_row, start):
    blocks = panel.shape[0] // BLOCK
    window = lax.dynamic_slice_in_dim(pattern_row, start, blocks)
    return panel * jnp.repeat(window, BLOCK).astype(panel.dtype)[:, None]


def left_factor(masked, inverse):
    return jnp.dot(masked.astype(jnp.float32), inverse, precision=lax.Precision.HIGHEST).astype(jnp.bfloat16)


def source_table(mapping, positions, parent_blocks):
    each = mapping.shape[0] // positions
    width = parent_blocks // (2 * positions)
    target = jnp.arange(parent_blocks, dtype=jnp.int32).reshape(2, positions, width)
    hit = mapping.reshape(1, positions, 1, each) == target[..., None]
    return jnp.sum(jnp.where(hit, jnp.arange(1, each + 1, dtype=jnp.int32), 0), axis=-1) - 1


def after(array, *earlier):
    return lax.optimization_barrier((array,) + earlier)[0]


def in_hbm(array):
    return pltpu.with_memory_space_constraint(array, pltpu.MemorySpace.HBM)


def assemble_group(at, positions, cols, each, width, table, place, lefts, own_set, other_set, own, other, trailing, previous):
    rows = own.shape[0]
    span = each * BLOCK
    wide = width * BLOCK
    row_blocks = rows // BLOCK
    zero = row_blocks * each

    def kernel(table_ref, place_ref, lefts_ref, own_set_ref, other_set_ref, own_ref, other_ref, trailing_ref, *rest):
        out_ref, schur_ref = rest[-2:]
        half = pl.program_id(0)
        own_half = place_ref[0]
        position = place_ref[1]

        def source(child, which_half, window, k):
            return table_ref[((child * 2 + which_half) * positions + window) * width + k]

        def panel_piece(child, j, which):
            if child == 0:
                return own_set_ref[j, which]
            return other_set_ref[(place_ref[3] + cols - j) % cols, which]

        @pl.when(half == 0)
        def _():
            for child, piece in enumerate((own_ref, other_ref)):
                for j in range(cols):
                    update = lax.dot_general(
                        lefts_ref[child], panel_piece(child, j, 0), (((1,), (1,)), ((), ())),
                        preferred_element_type=jnp.float32,
                    )
                    schur = (piece[:, j * span:(j + 1) * span].astype(jnp.float32) - update).astype(jnp.bfloat16)
                    for r in range(row_blocks):
                        for c in range(each):
                            schur_ref[child, j, r * each + c] = schur[r * BLOCK:(r + 1) * BLOCK, c * BLOCK:(c + 1) * BLOCK]
                    schur_ref[child, j, zero] = jnp.zeros((BLOCK, BLOCK), jnp.bfloat16)

        def emit(child_of_half):
            for j in range(cols):
                window = place_ref[2] + j
                update = lax.dot_general(
                    lefts_ref[2], panel_piece(child_of_half, j, 1), (((1,), (1,)), ((), ())),
                    preferred_element_type=jnp.float32,
                )
                base = trailing_ref[:, j * wide:(j + 1) * wide].astype(jnp.float32) - update
                for a in range(row_blocks):
                    for k in range(width):
                        blocks = []
                        for child in range(2):
                            r = source(child, own_half, position, a)
                            c = source(child, half, window, k)
                            which = jnp.where((r >= 0) & (c >= 0), r * each + c, zero)
                            blocks.append(schur_ref[child, j, which])
                        total = (blocks[0] + blocks[1]).astype(jnp.float32)
                        piece = base[a * BLOCK:(a + 1) * BLOCK, k * BLOCK:(k + 1) * BLOCK] + total
                        at_column = j * wide + k * BLOCK
                        out_ref[a * BLOCK:(a + 1) * BLOCK, at_column:at_column + BLOCK] = piece.astype(jnp.bfloat16)

        pl.when(half == own_half)(lambda: emit(0))
        pl.when(half != own_half)(lambda: emit(1))

    halves = positions // cols
    in_specs = [
        pl.BlockSpec(lefts.shape, lambda h, t, p: (0, 0, 0)),
        pl.BlockSpec((cols,) + own_set.shape[1:], lambda h, t, p: (p[2] // cols, 0, 0, 0)),
        pl.BlockSpec(other_set.shape, lambda h, t, p: (0, 0, 0, 0)),
        pl.BlockSpec((rows, cols * span), lambda h, t, p: (0, p[2] // cols)),
        pl.BlockSpec((rows, cols * span), lambda h, t, p: (0, at)),
        pl.BlockSpec((rows, cols * wide), lambda h, t, p: (0, h * halves + p[2] // cols)),
    ]
    operands = [lefts, in_hbm(own_set), in_hbm(other_set), in_hbm(own), in_hbm(other), in_hbm(trailing)]
    aliases = {}
    if previous is not None:
        in_specs.append(pl.BlockSpec(memory_space=pl.ANY))
        operands.append(previous)
        aliases = {len(operands) + 1: 0}
    windows = cols * rows
    return pl.pallas_call(
        kernel,
        grid_spec=pltpu.PrefetchScalarGridSpec(
            num_scalar_prefetch=2,
            grid=(2,),
            in_specs=in_specs,
            out_specs=pl.BlockSpec((rows, cols * wide), lambda h, t, p: (0, h * halves + p[2] // cols)),
            scratch_shapes=[pltpu.VMEM((2, cols, zero + 1, BLOCK, BLOCK), jnp.bfloat16)],
        ),
        out_shape=jax.ShapeDtypeStruct(trailing.shape, jnp.bfloat16),
        input_output_aliases=aliases,
        name="assemble",
        cost_estimate=pl.CostEstimate(
            flops=4 * windows * lefts.shape[2] * (span + wide),
            bytes_accessed=4 * windows * (span + 2 * wide) + 2 * (2 * other_set.size + lefts.size),
            transcendentals=0,
        ),
        compiler_params=pltpu.CompilerParams(vmem_limit_bytes=48 * 1024 * 1024),
    )(table, place, *operands)


def local(
    child_panel,
    child_inverse,
    child_trailing,
    child_pattern,
    child_map,
    parent_panel,
    parent_inverse,
    parent_trailing,
    parent_pattern,
):
    plane = ("row", "col")
    positions = lax.axis_size(plane)
    cols = lax.axis_size("col")
    row = lax.axis_index("row")
    col = lax.axis_index("col")
    position = lax.axis_index(plane)
    cube_index = lax.axis_index("cube")
    half_bit = cube_index % 2
    parent = cube_index // 2
    parent_blocks = parent_pattern.shape[1]
    each = child_map.shape[1] // positions
    width = parent_blocks // (2 * positions)
    own = child_trailing[0]
    trailing = parent_trailing[0]
    rows = own.shape[0]
    span = each * BLOCK

    own_child = masked_rows(child_panel[0], child_pattern[0], position * each)
    pattern_row = lax.dynamic_index_in_dim(parent_pattern, parent, 0, keepdims=False)
    own_parent = masked_rows(parent_panel[0], pattern_row, half_bit * (parent_blocks // 2) + position * width)
    own_piece = jnp.stack([own_child, own_parent])
    other_piece = swap(own_piece, "cube", 0)

    child_left = left_factor(own_child, child_inverse[0])
    parent_left = left_factor(own_parent, lax.dynamic_index_in_dim(parent_inverse, parent, 0, keepdims=False))
    other_left = swap(child_left, "cube", 0)
    lefts = jnp.stack([child_left, other_left, parent_left])

    def own_columns(deltas):
        parts = [lax.dynamic_slice_in_dim(own, (row ^ delta) * cols * span, cols * span, 1) for delta in deltas]
        return parts[0] if len(parts) == 1 else jnp.concatenate(parts, axis=1)

    own_set = lax.all_gather(own_piece, plane, axis=0, tiled=False)

    early = swap(after(own_columns([0, 1, 2]), other_piece), "cube", 0)
    late = swap(own_columns([3]), "cube", 0)

    shifted = [shift(other_piece, "col", j) for j in range(1, cols)]
    across = [swap(other_piece, "row", 1)]
    across.append(swap(after(shifted[0], across[0]), "row", 1))
    across.append(swap(shifted[1], "row", 1))
    across.append(swap(after(shifted[2], across[1]), "row", 1))
    near = jnp.stack([other_piece] + shifted)
    far = jnp.stack(across)
    other_sets = [near, swap(near, "row", 0), far, swap(after(far, early), "row", 0)]

    own_map = lax.dynamic_index_in_dim(child_map, cube_index, 0, keepdims=False)
    other_map = lax.dynamic_index_in_dim(child_map, cube_index ^ 1, 0, keepdims=False)
    table = jnp.stack([source_table(m, positions, parent_blocks) for m in (own_map, other_map)]).reshape(-1)

    result = None
    for delta, (other, at) in enumerate(((early, 0), (early, 1), (early, 2), (late, 0))):
        place = jnp.stack([half_bit, position, (row ^ delta) * cols, col]).astype(jnp.int32)
        result = assemble_group(
            at, positions, cols, each, width, table, place, lefts,
            own_set, other_sets[delta], own, other, trailing, result,
        )
    return result[None]


def solution(mesh):
    in_specs = (
        P("cube", ("row", "col"), None),
        P("cube", None, None),
        P("cube", ("row", "col"), None),
        P("cube", None),
        P(),
        P("cube", ("row", "col"), None),
        P(),
        P("cube", ("row", "col"), None),
        P(),
    )
    out_specs = P("cube", ("row", "col"), None)
    return jax.shard_map(local, mesh=mesh, in_specs=in_specs, out_specs=out_specs, check_vma=False)
```

```python
import jax
import jax.numpy as jnp
from jax import lax
from jax.experimental import pallas as pl
from jax.experimental.pallas import tpu as pltpu
from jax.sharding import PartitionSpec as P

BLOCK = 128


def swap(array, axis, bit):
    return lax.ppermute(array, axis, [(i, i ^ 1 << bit) for i in range(lax.axis_size(axis))])


def shift(array, axis, by):
    extent = lax.axis_size(axis)
    return lax.ppermute(array, axis, [(i, (i + by) % extent) for i in range(extent)])


def masked_rows(panel, pattern_row, start):
    blocks = panel.shape[0] // BLOCK
    window = lax.dynamic_slice_in_dim(pattern_row, start, blocks)
    return panel * jnp.repeat(window, BLOCK).astype(panel.dtype)[:, None]


def left_factor(masked, inverse):
    return jnp.dot(masked.astype(jnp.float32), inverse, precision=lax.Precision.HIGHEST).astype(jnp.bfloat16)


def source_table(mapping, positions, parent_blocks):
    each = mapping.shape[0] // positions
    width = parent_blocks // (2 * positions)
    target = jnp.arange(parent_blocks, dtype=jnp.int32).reshape(2, positions, width)
    hit = mapping.reshape(1, positions, 1, each) == target[..., None]
    return jnp.sum(jnp.where(hit, jnp.arange(1, each + 1, dtype=jnp.int32), 0), axis=-1) - 1


def ring(piece):
    extent = lax.axis_size("col")
    held = [piece]
    for _ in range(extent - 2):
        held.append(shift(held[-1], "col", 1))
    return held + [shift(piece, "col", extent - 1)]


def after(array, *earlier):
    return lax.optimization_barrier((array,) + earlier)[0]


def in_hbm(array):
    return pltpu.with_memory_space_constraint(array, pltpu.MemorySpace.HBM)


def assemble_group(at, positions, cols, each, width, table, place, lefts, own_set, other_set, own, other, trailing, previous):
    rows = own.shape[0]
    span = each * BLOCK
    wide = width * BLOCK
    row_blocks = rows // BLOCK
    zero = row_blocks * each

    def kernel(table_ref, place_ref, lefts_ref, own_set_ref, other_set_ref, own_ref, other_ref, trailing_ref, *rest):
        out_ref, schur_ref = rest[-2:]
        half = pl.program_id(0)
        own_half = place_ref[0]
        position = place_ref[1]

        def source(child, which_half, window, k):
            return table_ref[((child * 2 + which_half) * positions + window) * width + k]

        def panel_piece(child, j, which):
            held = own_set_ref if child == 0 else other_set_ref
            return held[(place_ref[3] + cols - j) % cols, which]

        @pl.when(half == 0)
        def _():
            for child, piece in enumerate((own_ref, other_ref)):
                for j in range(cols):
                    update = lax.dot_general(
                        lefts_ref[child], panel_piece(child, j, 0), (((1,), (1,)), ((), ())),
                        preferred_element_type=jnp.float32,
                    )
                    schur = (piece[:, j * span:(j + 1) * span].astype(jnp.float32) - update).astype(jnp.bfloat16)
                    for r in range(row_blocks):
                        for c in range(each):
                            schur_ref[child, j, r * each + c] = schur[r * BLOCK:(r + 1) * BLOCK, c * BLOCK:(c + 1) * BLOCK]
                    schur_ref[child, j, zero] = jnp.zeros((BLOCK, BLOCK), jnp.bfloat16)

        def emit(child_of_half):
            for j in range(cols):
                window = place_ref[2] + j
                update = lax.dot_general(
                    lefts_ref[2], panel_piece(child_of_half, j, 1), (((1,), (1,)), ((), ())),
                    preferred_element_type=jnp.float32,
                )
                base = trailing_ref[:, j * wide:(j + 1) * wide].astype(jnp.float32) - update
                for a in range(row_blocks):
                    for k in range(width):
                        blocks = []
                        for child in range(2):
                            r = source(child, own_half, position, a)
                            c = source(child, half, window, k)
                            which = jnp.where((r >= 0) & (c >= 0), r * each + c, zero)
                            blocks.append(schur_ref[child, j, which])
                        total = (blocks[0] + blocks[1]).astype(jnp.float32)
                        piece = base[a * BLOCK:(a + 1) * BLOCK, k * BLOCK:(k + 1) * BLOCK] + total
                        at_column = j * wide + k * BLOCK
                        out_ref[a * BLOCK:(a + 1) * BLOCK, at_column:at_column + BLOCK] = piece.astype(jnp.bfloat16)

        pl.when(half == own_half)(lambda: emit(0))
        pl.when(half != own_half)(lambda: emit(1))

    halves = positions // cols
    in_specs = [
        pl.BlockSpec(lefts.shape, lambda h, t, p: (0, 0, 0)),
        pl.BlockSpec(own_set.shape, lambda h, t, p: (0, 0, 0, 0)),
        pl.BlockSpec(other_set.shape, lambda h, t, p: (0, 0, 0, 0)),
        pl.BlockSpec((rows, cols * span), lambda h, t, p: (0, p[2] // cols)),
        pl.BlockSpec((rows, cols * span), lambda h, t, p: (0, at)),
        pl.BlockSpec((rows, cols * wide), lambda h, t, p: (0, h * halves + p[2] // cols)),
    ]
    operands = [lefts, in_hbm(own_set), in_hbm(other_set), in_hbm(own), in_hbm(other), in_hbm(trailing)]
    aliases = {}
    if previous is not None:
        in_specs.append(pl.BlockSpec(memory_space=pl.ANY))
        operands.append(previous)
        aliases = {len(operands) + 1: 0}
    windows = cols * rows
    return pl.pallas_call(
        kernel,
        grid_spec=pltpu.PrefetchScalarGridSpec(
            num_scalar_prefetch=2,
            grid=(2,),
            in_specs=in_specs,
            out_specs=pl.BlockSpec((rows, cols * wide), lambda h, t, p: (0, h * halves + p[2] // cols)),
            scratch_shapes=[pltpu.VMEM((2, cols, zero + 1, BLOCK, BLOCK), jnp.bfloat16)],
        ),
        out_shape=jax.ShapeDtypeStruct(trailing.shape, jnp.bfloat16),
        input_output_aliases=aliases,
        name="assemble",
        cost_estimate=pl.CostEstimate(
            flops=4 * windows * lefts.shape[2] * (span + wide),
            bytes_accessed=4 * windows * (span + 2 * wide) + 2 * (2 * other_set.size + lefts.size),
            transcendentals=0,
        ),
        compiler_params=pltpu.CompilerParams(vmem_limit_bytes=48 * 1024 * 1024),
    )(table, place, *operands)


def local(
    child_panel,
    child_inverse,
    child_trailing,
    child_pattern,
    child_map,
    parent_panel,
    parent_inverse,
    parent_trailing,
    parent_pattern,
):
    plane = ("row", "col")
    positions = lax.axis_size(plane)
    cols = lax.axis_size("col")
    row = lax.axis_index("row")
    col = lax.axis_index("col")
    position = lax.axis_index(plane)
    cube_index = lax.axis_index("cube")
    half_bit = cube_index % 2
    parent = cube_index // 2
    parent_blocks = parent_pattern.shape[1]
    each = child_map.shape[1] // positions
    width = parent_blocks // (2 * positions)
    own = child_trailing[0]
    trailing = parent_trailing[0]
    rows = own.shape[0]
    span = each * BLOCK

    own_child = masked_rows(child_panel[0], child_pattern[0], position * each)
    pattern_row = lax.dynamic_index_in_dim(parent_pattern, parent, 0, keepdims=False)
    own_parent = masked_rows(parent_panel[0], pattern_row, half_bit * (parent_blocks // 2) + position * width)
    own_piece = jnp.stack([own_child, own_parent])
    other_piece = swap(own_piece, "cube", 0)

    child_left = left_factor(own_child, child_inverse[0])
    parent_left = left_factor(own_parent, lax.dynamic_index_in_dim(parent_inverse, parent, 0, keepdims=False))
    other_left = swap(child_left, "cube", 0)
    lefts = jnp.stack([child_left, other_left, parent_left])

    def own_columns(deltas):
        parts = [lax.dynamic_slice_in_dim(own, (row ^ delta) * cols * span, cols * span, 1) for delta in deltas]
        return parts[0] if len(parts) == 1 else jnp.concatenate(parts, axis=1)

    early = swap(after(own_columns([0, 1, 2]), other_piece, other_left), "cube", 0)
    late = swap(own_columns([3]), "cube", 0)

    pieces = (own_piece, other_piece)
    along = [ring(piece) for piece in pieces]
    across = [[None] * cols, [None] * cols]
    done = []
    for which, j in ((0, 0), (0, 1), (1, 0), (0, 3), (1, 1), (0, 2), (1, 3), (1, 2)):
        needs = done[-2:-1]
        across[which][j] = swap(after(along[which][j], *needs), "row", 1)
        done.append(across[which][j])
    sets = []
    for near, far in zip(along, across):
        near, far = jnp.stack(near), jnp.stack(far)
        sets.append([near, swap(near, "row", 0), far, swap(far, "row", 0)])
    own_sets, other_sets = sets

    own_map = lax.dynamic_index_in_dim(child_map, cube_index, 0, keepdims=False)
    other_map = lax.dynamic_index_in_dim(child_map, cube_index ^ 1, 0, keepdims=False)
    table = jnp.stack([source_table(m, positions, parent_blocks) for m in (own_map, other_map)]).reshape(-1)

    result = None
    for delta, (other, at) in enumerate(((early, 0), (early, 1), (early, 2), (late, 0))):
        place = jnp.stack([half_bit, position, (row ^ delta) * cols, col]).astype(jnp.int32)
        result = assemble_group(
            at, positions, cols, each, width, table, place, lefts,
            own_sets[delta], other_sets[delta], own, other, trailing, result,
        )
    return result[None]


def solution(mesh):
    in_specs = (
        P("cube", ("row", "col"), None),
        P("cube", None, None),
        P("cube", ("row", "col"), None),
        P("cube", None),
        P(),
        P("cube", ("row", "col"), None),
        P(),
        P("cube", ("row", "col"), None),
        P(),
    )
    out_specs = P("cube", ("row", "col"), None)
    return jax.shard_map(local, mesh=mesh, in_specs=in_specs, out_specs=out_specs, check_vma=False)
```

```python
import jax
import jax.numpy as jnp
from jax import lax
from jax.experimental import pallas as pl
from jax.experimental.pallas import tpu as pltpu
from jax.sharding import PartitionSpec as P

BLOCK = 128


def swap(array, axis, bit):
    return lax.ppermute(array, axis, [(i, i ^ 1 << bit) for i in range(lax.axis_size(axis))])


def shift(array, axis, by):
    extent = lax.axis_size(axis)
    return lax.ppermute(array, axis, [(i, (i + by) % extent) for i in range(extent)])


def masked_pair(child, parent, child_pattern, parent_pattern, starts):
    rows, pivots = child.shape
    blocks = rows // BLOCK

    def kernel(starts_ref, child_pattern_ref, parent_pattern_ref, child_ref, parent_ref, out_ref):
        for i in range(blocks):
            at = slice(i * BLOCK, (i + 1) * BLOCK)
            for which, (source_ref, flag) in enumerate((
                (child_ref, child_pattern_ref[0, starts_ref[0] + i]),
                (parent_ref, parent_pattern_ref[starts_ref[1], starts_ref[2] + i]),
            )):
                here = source_ref[at]
                out_ref[which, at] = jnp.where(flag != 0, here, jnp.zeros_like(here))

    smem = pl.BlockSpec(memory_space=pltpu.SMEM)
    vmem = pl.BlockSpec(memory_space=pltpu.VMEM)
    return pl.pallas_call(
        kernel,
        in_specs=[smem, smem, smem, vmem, vmem],
        out_specs=vmem,
        out_shape=jax.ShapeDtypeStruct((2, rows, pivots), jnp.bfloat16),
        name="masked",
    )(starts, child_pattern, parent_pattern, child, parent)


def left_factor(masked, inverse):
    return jnp.dot(masked.astype(jnp.float32), inverse, precision=lax.Precision.HIGHEST).astype(jnp.bfloat16)


def source_table(mapping, positions, parent_blocks):
    each = mapping.shape[0] // positions
    width = parent_blocks // (2 * positions)
    target = jnp.arange(parent_blocks, dtype=jnp.int32).reshape(2, positions, width)
    hit = mapping.reshape(1, positions, 1, each) == target[..., None]
    return jnp.sum(jnp.where(hit, jnp.arange(1, each + 1, dtype=jnp.int32), 0), axis=-1) - 1


def ring(piece):
    extent = lax.axis_size("col")
    held = [piece]
    for _ in range(extent - 2):
        held.append(shift(held[-1], "col", 1))
    return held + [shift(piece, "col", extent - 1)]


def after(array, *earlier):
    return lax.optimization_barrier((array,) + earlier)[0]


def in_hbm(array):
    return pltpu.with_memory_space_constraint(array, pltpu.MemorySpace.HBM)


def assemble_group(at, positions, cols, each, width, table, place, lefts, own_set, other_set, own, other, trailing, previous):
    rows = own.shape[0]
    span = each * BLOCK
    wide = width * BLOCK
    row_blocks = rows // BLOCK
    zero = row_blocks * each

    def kernel(table_ref, place_ref, lefts_ref, own_set_ref, other_set_ref, own_ref, other_ref, trailing_ref, *rest):
        out_ref, schur_ref = rest[-2:]
        half = pl.program_id(0)
        own_half = place_ref[0]
        position = place_ref[1]

        def source(child, which_half, window, k):
            return table_ref[((child * 2 + which_half) * positions + window) * width + k]

        def panel_piece(child, j, which):
            held = own_set_ref if child == 0 else other_set_ref
            return held[(place_ref[3] + cols - j) % cols, which]

        @pl.when(half == 0)
        def _():
            for child, piece in enumerate((own_ref, other_ref)):
                for j in range(cols):
                    update = lax.dot_general(
                        lefts_ref[child], panel_piece(child, j, 0), (((1,), (1,)), ((), ())),
                        preferred_element_type=jnp.float32,
                    )
                    schur = (piece[:, j * span:(j + 1) * span].astype(jnp.float32) - update).astype(jnp.bfloat16)
                    for r in range(row_blocks):
                        for c in range(each):
                            schur_ref[child, j, r * each + c] = schur[r * BLOCK:(r + 1) * BLOCK, c * BLOCK:(c + 1) * BLOCK]
                    schur_ref[child, j, zero] = jnp.zeros((BLOCK, BLOCK), jnp.bfloat16)

        def emit(child_of_half):
            for j in range(cols):
                window = place_ref[2] + j
                update = lax.dot_general(
                    lefts_ref[2], panel_piece(child_of_half, j, 1), (((1,), (1,)), ((), ())),
                    preferred_element_type=jnp.float32,
                )
                base = trailing_ref[:, j * wide:(j + 1) * wide].astype(jnp.float32) - update
                for a in range(row_blocks):
                    for k in range(width):
                        blocks = []
                        for child in range(2):
                            r = source(child, own_half, position, a)
                            c = source(child, half, window, k)
                            which = jnp.where((r >= 0) & (c >= 0), r * each + c, zero)
                            blocks.append(schur_ref[child, j, which])
                        total = (blocks[0] + blocks[1]).astype(jnp.float32)
                        piece = base[a * BLOCK:(a + 1) * BLOCK, k * BLOCK:(k + 1) * BLOCK] + total
                        at_column = j * wide + k * BLOCK
                        out_ref[a * BLOCK:(a + 1) * BLOCK, at_column:at_column + BLOCK] = piece.astype(jnp.bfloat16)

        pl.when(half == own_half)(lambda: emit(0))
        pl.when(half != own_half)(lambda: emit(1))

    halves = positions // cols
    in_specs = [
        pl.BlockSpec(lefts.shape, lambda h, t, p: (0, 0, 0)),
        pl.BlockSpec(own_set.shape, lambda h, t, p: (0, 0, 0, 0)),
        pl.BlockSpec(other_set.shape, lambda h, t, p: (0, 0, 0, 0)),
        pl.BlockSpec((rows, cols * span), lambda h, t, p: (0, p[2] // cols)),
        pl.BlockSpec((rows, cols * span), lambda h, t, p: (0, at)),
        pl.BlockSpec((rows, cols * wide), lambda h, t, p: (0, h * halves + p[2] // cols)),
    ]
    operands = [lefts, own_set, other_set, in_hbm(own), other, in_hbm(trailing)]
    aliases = {}
    if previous is not None:
        in_specs.append(pl.BlockSpec(memory_space=pl.ANY))
        operands.append(previous)
        aliases = {len(operands) + 1: 0}
    windows = cols * rows
    return pl.pallas_call(
        kernel,
        grid_spec=pltpu.PrefetchScalarGridSpec(
            num_scalar_prefetch=2,
            grid=(2,),
            in_specs=in_specs,
            out_specs=pl.BlockSpec((rows, cols * wide), lambda h, t, p: (0, h * halves + p[2] // cols)),
            scratch_shapes=[pltpu.VMEM((2, cols, zero + 1, BLOCK, BLOCK), jnp.bfloat16)],
        ),
        out_shape=jax.ShapeDtypeStruct(trailing.shape, jnp.bfloat16),
        input_output_aliases=aliases,
        name="assemble",
        cost_estimate=pl.CostEstimate(
            flops=4 * windows * lefts.shape[2] * (span + wide),
            bytes_accessed=4 * windows * (span + 2 * wide) + 2 * (2 * other_set.size + lefts.size),
            transcendentals=0,
        ),
        compiler_params=pltpu.CompilerParams(vmem_limit_bytes=48 * 1024 * 1024),
    )(table, place, *operands)


def local(
    child_panel,
    child_inverse,
    child_trailing,
    child_pattern,
    child_map,
    parent_panel,
    parent_inverse,
    parent_trailing,
    parent_pattern,
):
    plane = ("row", "col")
    positions = lax.axis_size(plane)
    cols = lax.axis_size("col")
    row = lax.axis_index("row")
    col = lax.axis_index("col")
    position = lax.axis_index(plane)
    cube_index = lax.axis_index("cube")
    half_bit = cube_index % 2
    parent = cube_index // 2
    parent_blocks = parent_pattern.shape[1]
    each = child_map.shape[1] // positions
    width = parent_blocks // (2 * positions)
    own = child_trailing[0]
    trailing = parent_trailing[0]
    rows = own.shape[0]
    span = each * BLOCK

    starts = jnp.stack([position * each, parent, half_bit * (parent_blocks // 2) + position * width]).astype(jnp.int32)
    own_piece = masked_pair(child_panel[0], parent_panel[0], child_pattern, parent_pattern, starts)
    own_child, own_parent = own_piece[0], own_piece[1]
    other_piece = swap(own_piece, "cube", 0)

    child_left = left_factor(own_child, child_inverse[0])
    parent_left = left_factor(own_parent, lax.dynamic_index_in_dim(parent_inverse, parent, 0, keepdims=False))
    other_left = swap(child_left, "cube", 0)
    lefts = jnp.stack([child_left, other_left, parent_left])

    def own_columns(deltas):
        parts = [lax.dynamic_slice_in_dim(own, (row ^ delta) * cols * span, cols * span, 1) for delta in deltas]
        return parts[0] if len(parts) == 1 else jnp.concatenate(parts, axis=1)

    early = swap(after(own_columns([0, 1, 2]), other_piece, other_left), "cube", 0)
    late = swap(own_columns([3]), "cube", 0)

    pieces = (own_piece, other_piece)
    along = [ring(piece) for piece in pieces]
    across = [[None] * cols, [None] * cols]
    done = []
    for which, j in ((0, 0), (0, 1), (1, 0), (0, 3), (1, 1), (0, 2), (1, 3), (1, 2)):
        needs = done[-2:-1] + ([lefts] if (which, j) == (1, 2) else [])
        across[which][j] = swap(after(along[which][j], *needs), "row", 1)
        done.append(across[which][j])
    sets = []
    for near, far in zip(along, across):
        near, far = jnp.stack(near), jnp.stack(far)
        sets.append([near, swap(near, "row", 0), far, swap(far, "row", 0)])
    own_sets, other_sets = sets

    own_map = lax.dynamic_index_in_dim(child_map, cube_index, 0, keepdims=False)
    other_map = lax.dynamic_index_in_dim(child_map, cube_index ^ 1, 0, keepdims=False)
    table = jnp.stack([source_table(m, positions, parent_blocks) for m in (own_map, other_map)]).reshape(-1)

    result = None
    for delta, (other, at) in enumerate(((early, 0), (early, 1), (early, 2), (late, 0))):
        place = jnp.stack([half_bit, position, (row ^ delta) * cols, col]).astype(jnp.int32)
        result = assemble_group(
            at, positions, cols, each, width, table, place, lefts,
            own_sets[delta], other_sets[delta], own, other, trailing, result,
        )
    return result[None]


def solution(mesh):
    in_specs = (
        P("cube", ("row", "col"), None),
        P("cube", None, None),
        P("cube", ("row", "col"), None),
        P("cube", None),
        P(),
        P("cube", ("row", "col"), None),
        P(),
        P("cube", ("row", "col"), None),
        P(),
    )
    out_specs = P("cube", ("row", "col"), None)
    return jax.shard_map(local, mesh=mesh, in_specs=in_specs, out_specs=out_specs, check_vma=False)
```
